32 devices in a mesh: groups: 2 (over x), ta: 16 (over z, y, core).
Axes of the slice: x: 2, y: 2, z: 4, core: 2. Of those that a mesh axis runs over, the one named last changes fastest.
Arguments:
- out_field: float32 [16, 64, 1024], P(None, ('groups', 'ta')), parts along dimension 1, may hold values from -6 to 6
- out_cot: float32 [16, 64, 1024], P(None, ('groups', 'ta')), parts along dimension 1, may hold values from -6 to 6
- jac_cot: float32 [64, 1024], P(('groups', 'ta')), parts along dimension 0, may hold values from -6 to 6
- mask: int32 [64, 1024], P(('groups', 'ta')), parts along dimension 0, may hold values 0 or 1
- perm: int32 [16], replicated, may hold values from 0 to 15, each once
- lower_param: float32 [16, 16], replicated, may hold values from -0.6 to 0.6
- upper_param: float32 [16, 16], replicated, may hold values from -0.6 to 0.6
- log_scale: float32 [16], replicated, may hold values from -0.3 to 0.3
- kern1: bfloat16 [81, 32, 16], replicated, may hold values from -0.15625 to 0.15625
- bias1: float32 [32], replicated, may hold values from -3 to 3
- kern2: bfloat16 [81, 32, 32], replicated, may hold values from -0.125 to 0.125
- bias2: float32 [32], replicated, may hold values from -2 to 2
Outputs:
- field_in: float32 [16, 64, 1024], P(None, ('groups', 'ta')), parts along dimension 1
- field_cot: float32 [16, 64, 1024], P(None, ('groups', 'ta')), parts along dimension 1
- grad_kern1: float32 [162, 32, 16], P('groups'), parts along dimension 0
- grad_bias1: float32 [64], P('groups'), parts along dimension 0
- grad_kern2: float32 [162, 32, 32], P('groups'), parts along dimension 0
- grad_bias2: float32 [64], P('groups'), parts along dimension 0
- grad_lower: float32 [32, 16], P('groups'), parts along dimension 0
- grad_upper: float32 [32, 16], P('groups'), parts along dimension 0
- grad_logs: float32 [32], P('groups'), parts along dimension 0
The draws below stay inside these ranges and needn't reach their ends.
There are 2 independent parts, one for each index of `groups`. The reference program is written for one: setup_inputs(seed, part) draws one part's arguments, and reference() takes and returns one part's arrays. A program takes and returns all parts, laid end to end along the dimension named above; an argument that names none is the same for every part. Nothing has to cross between parts.
Inputs may be any that keep to these rules, and one draw needn't show every extreme that they name: `perm`: each of 0 to 15 exactly once.
All inputs are finite; a program needn't handle non-finite values. No bound on the sum of `mask` on one device may be relied on, other than what follows from the above.
Results may differ from the reference program's by a relative error of at most 0.0076.
Values may be sent and summed in bfloat16 or wider, within the bound.
No kernel may reach another device: no remote copies, remote signals or barrier semaphores. Data moves between devices by JAX's collectives and lax.ppermute only.
A program may use at most 64 MiB of HBM per device.

```python
import math
import jax
import jax.numpy as jnp
from jax import lax

C = 16
HID = 32
LX = 8
LY = 8
LZ = 16
S = 1024
NT = 32
SITES_ALL = 32768


def with_ends(array, key, smallest, high):
    extent = array.shape
    place = [jax.random.randint(jax.random.fold_in(key, axis), (), 0, extent[axis]) for axis in range(len(extent))]
    array = array.at[tuple(place)].set(smallest)
    longest = extent.index(max(extent))
    place[longest] = (place[longest] + 1) % extent[longest]
    return array.at[tuple(place)].set(high)


def block_levels(own_key, extent, split, low, top_value):
    factor_of = 1.0
    for position, parts in split:
        heights = jax.random.uniform(jax.random.fold_in(jax.random.fold_in(own_key, 6), position), (parts,), jnp.float32, low / len(split), top_value / len(split))
        factor_of = factor_of * jnp.repeat(jnp.exp(heights), extent[position] // parts).reshape((-1,) + (1,) * (len(extent) - 1 - position))
    return factor_of


def centred(rng, extent, spread, limit, pieces=(), kind=jnp.bfloat16):
    factor_of = block_levels(rng, extent, pieces, -0.22, 0.18) if pieces else 1.0
    array = jax.random.normal(rng, extent, jnp.float32) * spread * factor_of
    return jnp.minimum(jnp.maximum(array, -limit), limit).astype(kind)


def setup_inputs(seed: int = 0, part: int = 0) -> dict:
    key_of = jax.random.split(jax.random.key(seed), 13)
    own_keys = jax.random.split(jax.random.fold_in(key_of[12], part), 13)
    return {
        "out_field": centred(own_keys[0], (C, NT, S), 1.0, 6.0, ((1, 16),), jnp.float32),
        "out_cot": centred(own_keys[1], (C, NT, S), 1.0, 6.0, ((1, 16),), jnp.float32),
        "jac_cot": centred(own_keys[2], (NT, S), 1.0, 6.0, ((0, 16),), jnp.float32),
        "mask": with_ends((jax.random.randint(own_keys[3], (NT, S), 0, 2) < 1).astype(jnp.int32), jax.random.fold_in(own_keys[3], 1), 0, 1),
        "perm": jax.random.permutation(key_of[4], C).astype(jnp.int32),
        "lower_param": centred(key_of[5], (C, C), 0.15, 0.6, (), jnp.float32),
        "upper_param": centred(key_of[6], (C, C), 0.15, 0.6, (), jnp.float32),
        "log_scale": jnp.clip(jax.random.uniform(key_of[7], (C,), jnp.float32, -0.3, 0.3), -0.3, 0.3),
        "kern1": centred(key_of[8], (81, HID, C), (81 * C) ** -0.5, 0.15625),
        "bias1": centred(key_of[9], (HID,), 0.5, 3.0, (), jnp.float32),
        "kern2": centred(key_of[10], (81, 2 * C, HID), (81 * HID) ** -0.5, 0.125),
        "bias2": centred(key_of[11], (2 * C,), 0.3, 2.0, (), jnp.float32),
    }


HIGH = lax.Precision.HIGHEST

def nilpotent_inverse(nilpart):
    count = nilpart.shape[0]
    eye = jnp.eye(count, dtype=jnp.float32)
    result = eye - nilpart
    power = jnp.dot(nilpart, nilpart, precision=HIGH)
    span = 2
    while span < count:
        result = jnp.dot(result, eye + power, precision=HIGH)
        power = jnp.dot(power, power, precision=HIGH)
        span = span * 2
    return result

def lower_inverse(lower_tri):
    return nilpotent_inverse(jnp.tril(lower_tri, -1))

def upper_inverse(upper_tri):
    diag_vals = jnp.diagonal(upper_tri)
    scaled = jnp.triu(upper_tri, 1) / diag_vals[:, None]
    return nilpotent_inverse(scaled) * (1.0 / diag_vals)[None, :]

def all_offsets():
    listing = []
    for t_off in (-1, 0, 1):
        for x_off in (-1, 0, 1):
            for y_off in (-1, 0, 1):
                for z_off in (-1, 0, 1):
                    listing.append((t_off, x_off, y_off, z_off))
    return listing

def roll_field(values, offsets):
    return jnp.roll(values, shift=(-offsets[0], -offsets[1], -offsets[2], -offsets[3]), axis=(1, 2, 3, 4))

def conv_ref(values, kernel):
    kernel_f = kernel.astype(jnp.float32)
    total = None
    for tap_id, offsets in enumerate(all_offsets()):
        term = jnp.einsum('oi,itxyz->otxyz', kernel_f[tap_id], roll_field(values, offsets), precision=HIGH)
        total = term if total is None else total + term
    return total

def grads_ref(cotangent, values):
    blocks = []
    for offsets in all_offsets():
        blocks.append(jnp.einsum('otxyz,itxyz->oi', cotangent, roll_field(values, offsets), precision=HIGH))
    return jnp.stack(blocks)

def reference(out_field, out_cot, jac_cot, mask, perm, lower_param, upper_param, log_scale, kern1, bias1, kern2, bias2):
    chans = out_field.shape[0]
    slices = out_field.shape[1]
    shape5 = (chans, slices, LX, LY, LZ)
    eye = jnp.eye(chans, dtype=jnp.float32)
    permuter = (perm[:, None] == jnp.arange(chans, dtype=jnp.int32)[None, :]).astype(jnp.float32)
    lower_tri = jnp.tril(lower_param, -1) + eye
    upper_tri = jnp.triu(upper_param, 1) + jnp.diag(jnp.exp(log_scale))
    mixer = jnp.dot(jnp.dot(permuter, lower_tri, precision=HIGH), upper_tri, precision=HIGH)
    unmixer = jnp.dot(jnp.dot(upper_inverse(upper_tri), lower_inverse(lower_tri), precision=HIGH), permuter.T, precision=HIGH)
    flat_out = out_field.reshape(chans, -1)
    flat_coupled = jnp.dot(unmixer, flat_out, precision=HIGH)
    coupled = flat_coupled.reshape(shape5)
    keep = mask.reshape(shape5[1:]).astype(jnp.float32)[None]
    free_part = 1.0 - keep
    frozen = (keep * coupled).astype(jnp.bfloat16)
    frozen_f = frozen.astype(jnp.float32)
    hidden = jnp.tanh(conv_ref(frozen_f, kern1) + bias1[:, None, None, None, None]).astype(jnp.bfloat16)
    hidden_f = hidden.astype(jnp.float32)
    net_out = conv_ref(hidden_f, kern2) + bias2[:, None, None, None, None]
    scale_field = jnp.tanh(net_out[:chans])
    shift_field = net_out[chans:]
    field_in = keep * coupled + free_part * (coupled - shift_field) * jnp.exp(-scale_field)
    flat_cot = out_cot.reshape(chans, -1)
    coupled_cot = jnp.dot(mixer.T, flat_cot, precision=HIGH).reshape(shape5)
    mix_sum = jnp.dot(flat_cot, flat_coupled.T, precision=HIGH)
    jac_field = jac_cot.reshape(shape5[1:])[None]
    growth = jnp.exp(scale_field)
    scale_cot = free_part * (coupled_cot * field_in * growth + jac_field)
    net_cot = jnp.concatenate([scale_cot * (1.0 - scale_field * scale_field), free_part * coupled_cot], axis=0).astype(jnp.bfloat16)
    net_cot_f = net_cot.astype(jnp.float32)
    grad_k2 = grads_ref(net_cot_f, hidden_f)
    grad_b2 = lax.optimization_barrier(jnp.sum(net_cot_f, axis=(1, 2, 3, 4)))
    hidden_cot = conv_ref(net_cot_f, kern2[::-1].transpose(0, 2, 1))
    pre_cot = (hidden_cot * (1.0 - hidden_f * hidden_f)).astype(jnp.bfloat16)
    pre_cot_f = pre_cot.astype(jnp.float32)
    grad_k1 = grads_ref(pre_cot_f, frozen_f)
    grad_b1 = lax.optimization_barrier(jnp.sum(pre_cot_f, axis=(1, 2, 3, 4)))
    frozen_cot = conv_ref(pre_cot_f, kern1[::-1].transpose(0, 2, 1))
    field_cot = keep * (coupled_cot + frozen_cot) + free_part * coupled_cot * growth
    norm = 1.0 / math.sqrt(SITES_ALL)
    mix_grad = norm * mix_sum
    lower_full = jnp.dot(jnp.dot(permuter.T, mix_grad, precision=HIGH), upper_tri.T, precision=HIGH)
    upper_full = jnp.dot(lower_tri.T, jnp.dot(permuter.T, mix_grad, precision=HIGH), precision=HIGH)
    grad_lower = jnp.tril(lower_full, -1)
    grad_upper = jnp.triu(upper_full, 1)
    grad_logs = jnp.diagonal(upper_full) * jnp.exp(log_scale) + norm * jnp.sum(jac_cot)
    return (field_in.reshape(chans, slices, -1), field_cot.reshape(chans, slices, -1), norm * grad_k1, norm * grad_b1, norm * grad_k2, norm * grad_b2, grad_lower, grad_upper, grad_logs)
```

```python
import functools
import math

import jax
import jax.numpy as jnp
from jax import lax
from jax.experimental import pallas as pl
from jax.experimental.pallas import tpu as pltpu
from jax.sharding import PartitionSpec as P

LX = 8
LY = 8
LZ = 16
ROW = LY * LZ
PAD = (LX + 2) * ROW

HIGH = lax.Precision.HIGHEST
F32 = jnp.float32
BF16 = jnp.bfloat16


NN = (((1,), (0,)), ((), ()))
NT = (((1,), (1,)), ((), ()))
TN = (((0,), (0,)), ((), ()))


def exact(a, b, dims):
    return lax.dot_general(a, b, dims, precision=HIGH, preferred_element_type=F32)


def fast(a, b, dims):
    return lax.dot_general(a, b, dims, preferred_element_type=F32)


def vmem_call(kernel, out_shape, args, flops, scratch=()):
    spec = pl.BlockSpec(memory_space=pltpu.VMEM)
    moved = sum(a.size * a.dtype.itemsize for a in args)
    return pl.pallas_call(
        kernel,
        out_shape=out_shape,
        in_specs=[spec] * len(args),
        out_specs=jax.tree.map(lambda _: spec, out_shape),
        scratch_shapes=list(scratch),
        compiler_params=pltpu.CompilerParams(vmem_limit_bytes=40 << 20),
        cost_estimate=pl.CostEstimate(flops=flops, bytes_accessed=moved, transcendentals=0),
    )(*args)


def shape(dims, dtype=F32):
    return jax.ShapeDtypeStruct(dims, dtype)


def mix_parts(perm, lower, upper):
    count = lower.shape[0]
    row = lax.broadcasted_iota(jnp.int32, (count, count), 0)
    col = lax.broadcasted_iota(jnp.int32, (count, count), 1)
    perm_t = (row == perm).astype(F32)
    eye = (row == col).astype(F32)
    strict_low = jnp.where(row > col, lower, 0.0)
    strict_up = jnp.where(row < col, upper, 0.0)
    return perm_t, eye, strict_low, strict_up


def mix_kernel(steps, perm, lower, upper, logs_row, logs_col, out_field, out_cot, jac, mask,
               coupled, cot, pack_up, pack_down, edge_last, edge_first, mix_local):
    chans = lower.shape[0]
    perm_t, eye, strict_low, strict_up = mix_parts(perm[...], lower[...], upper[...])
    inv_diag = 1.0 / jnp.exp(logs_col[...])
    solve = perm_t
    for j in range(chans - 1):
        solve = solve - strict_low[:, j : j + 1] * solve[j : j + 1, :]
    solve = solve * inv_diag
    scaled = strict_up * inv_diag
    for j in range(chans - 1, 0, -1):
        solve = solve - scaled[:, j : j + 1] * solve[j : j + 1, :]
    upper_tri = strict_up + eye * jnp.exp(logs_row[...])
    low_up = exact(strict_low + eye, upper_tri, NN)
    low_up_t = exact(eye, low_up, NT)
    perm_mat_t = exact(low_up_t, perm_t, NN)

    def gather(ref):
        return jnp.concatenate(
            [
                ref[pl.ds(x * steps + t, chans, stride=LX * steps), :]
                for t in range(steps)
                for x in range(LX)
            ],
            axis=1,
        )

    cot_in = gather(out_cot)
    coupled_val = exact(solve, gather(out_field), NN)
    cot_val = exact(perm_mat_t, cot_in, NN)
    coupled[...] = coupled_val
    cot[...] = cot_val
    mix_local[...] = exact(cot_in, coupled_val, NT)
    keep = mask[...].astype(F32)
    span = LX * ROW
    for t in range(steps):
        block = coupled_val[:, t * span : (t + 1) * span].astype(BF16)
        pack_up[t * chans : (t + 1) * chans, :span] = block
        pack_down[t * chans : (t + 1) * chans, :span] = block
    top = steps * chans
    pack_up[top : top + chans, :span] = cot_val[:, (steps - 1) * span :].astype(BF16)
    pack_down[top : top + chans, :span] = cot_val[:, :span].astype(BF16)
    jac_val = jac[...]
    jac_hi = jac_val.astype(BF16)
    jac_lo = (jac_val - jac_hi.astype(F32)).astype(BF16)
    rows = LX * steps
    for pack in (pack_up, pack_down):
        pack[:rows, span:] = jac_hi
        pack[rows : 2 * rows, span:] = jac_lo
        pack[2 * rows : 3 * rows, span:] = keep.astype(BF16)
    for t, edge in ((steps - 1, edge_last), (0, edge_first)):
        for x in range(LX):
            at = t * span + x * ROW
            row = x * steps + t
            edge[:, x * ROW : (x + 1) * ROW] = (keep[row : row + 1] * coupled_val[:, at : at + ROW]).astype(BF16)


def weight_kernel(kern1, kern2, first, second, first_back, second_back):
    outs, hid = kern1.shape[2], kern1.shape[1]
    for a in range(3):
        for kern, forward, backward in ((kern1, first, first_back), (kern2, second, second_back)):
            o, i = kern.shape[1:]
            eye = (
                lax.broadcasted_iota(jnp.int32, (i, i), 0) == lax.broadcasted_iota(jnp.int32, (i, i), 1)
            ).astype(BF16)
            for j in range(27):
                forward[a * o : (a + 1) * o, j * i : (j + 1) * i] = kern[a * 27 + j]
            flat = jnp.concatenate([kern[a * 27 + j] for j in range(27)], axis=0)
            backward[a * i : (a + 1) * i, :] = fast(eye, flat, NT).astype(BF16)


def build_stack(stack, base, values, flip):
    chans = values.shape[0]
    tall = jnp.concatenate([values[:, x * ROW : (x + 1) * ROW] for x in range(LX)], axis=0)
    z = lax.broadcasted_iota(jnp.int32, tall.shape, 1) % LZ
    before = jnp.where(z == 0, pltpu.roll(tall, ROW - (LZ - 1), 1), pltpu.roll(tall, 1, 1))
    after = jnp.where(z == LZ - 1, pltpu.roll(tall, LZ - 1, 1), pltpu.roll(tall, ROW - 1, 1))
    for e, along_z in enumerate((before, tall, after)):
        for c, amount in enumerate((LZ, 0, ROW - LZ)):
            moved = pltpu.roll(along_z, amount, 1) if amount else along_z
            at = c * 3 + e
            at = (8 - at if flip else at) * chans
            for x in range(LX):
                block = moved[x * chans : (x + 1) * chans]
                spots = [x + 1] + ([LX + 1] if x == 0 else []) + ([0] if x == LX - 1 else [])
                for spot in spots:
                    stack[at : at + chans, base + spot * ROW : base + (spot + 1) * ROW] = block


WIDE = 256
PARTS = LX * ROW // WIDE


def taps(weights, stack, base, part, flip):
    order = (2, 1, 0) if flip else (0, 1, 2)
    start = base + part * WIDE
    block = jnp.concatenate([stack[:, start + b * ROW : start + b * ROW + WIDE] for b in order], axis=0)
    return fast(weights, block, NN)


def convolve(weights, stack, acc, count, outs, flip, finish):
    span = LX * ROW
    for q in range(count):
        for part in range(PARTS):
            all_taps = taps(weights, stack, q * PAD, part, flip)
            groups = [all_taps[a * outs : (a + 1) * outs] for a in range(3)]
            if flip:
                groups = groups[::-1]
            for a, group in enumerate(groups):
                p = q - a
                if 0 <= p <= count - 3:
                    where = slice(p * span + part * WIDE, p * span + (part + 1) * WIDE)
                    if a == 0:
                        acc[:, where] = group
                    elif a == 1:
                        acc[:, where] = acc[:, where] + group
                    else:
                        finish(p, part, acc[:, where] + group)


def main_kernel(steps, coupled, cot, jac, mask, from_prev, from_next, from_prev2, from_next2,
                first, second, second_back, bias1, bias2, mix_local,
                field_in, gated, pre_first, pre_last, packed,
                stack1, stack2, stack3, pre_pad, hidden, net, acc1, acc2, acc3, grad1, grad2):
    chans = coupled.shape[0]
    hid = bias1.shape[0]
    span = LX * ROW
    rows = LX * steps
    keep_own = mask[...].astype(F32)
    jac_own = jac[...]
    sides = {}
    for name, pack in (("prev", from_prev), ("next", from_next)):
        keep = pack[2 * rows : 3 * rows, span:].astype(F32)
        jac_side = pack[:rows, span:].astype(F32) + pack[rows : 2 * rows, span:].astype(F32)
        sides[name] = (pack, keep, jac_side)

    def row_of(block, t, x):
        return block[x * steps + t : x * steps + t + 1]

    def masked(values, keep, t):
        return jnp.concatenate(
            [(row_of(keep, t, x) * values[:, x * ROW : (x + 1) * ROW]).astype(BF16) for x in range(LX)], axis=1
        )

    first_w = first[...]
    second_w = second[...]
    back_w = second_back[...]
    slices = [from_prev2[...]]
    for t in range(steps):
        slices.append(masked(from_prev[t * chans : (t + 1) * chans, :span].astype(F32), sides["prev"][1], t))
    for t in range(steps):
        slices.append(masked(coupled[:, t * span : (t + 1) * span], keep_own, t))
    for t in range(steps):
        slices.append(masked(from_next[t * chans : (t + 1) * chans, :span].astype(F32), sides["next"][1], t))
    slices.append(from_next2[...])
    for q, values in enumerate(slices):
        build_stack(stack1, q * PAD, values, False)

    offset1 = bias1[...]

    def finish_hidden(p, part, value):
        hidden[:, p * span + part * WIDE : p * span + (part + 1) * WIDE] = jnp.tanh(value + offset1).astype(BF16)

    convolve(first_w, stack1, acc1, len(slices), hid, False, finish_hidden)
    hidden_count = len(slices) - 2
    for q in range(hidden_count):
        build_stack(stack2, q * PAD, hidden[:, q * span : (q + 1) * span], False)

    offset2 = bias2[...]
    net_count = hidden_count - 2
    sums = [jnp.zeros((2 * chans, WIDE), F32)]

    def finish_net(p, part, value):
        value = value + offset2
        scale = jnp.tanh(value[:chans])
        shift = value[chans:]
        lanes = slice(part * WIDE, (part + 1) * WIDE)
        own = 1 <= p <= steps
        if own:
            t = p - 1
            here = slice(t * span + part * WIDE, t * span + (part + 1) * WIDE)
            coupled_val, cot_val = coupled[:, here], cot[:, here]
            keep_rows, jac_rows = keep_own, jac_own
        else:
            pack, keep_rows, jac_rows = sides["prev" if p == 0 else "next"]
            t = steps - 1 if p == 0 else 0
            coupled_val = pack[t * chans : (t + 1) * chans, lanes].astype(F32)
            cot_val = pack[steps * chans : (steps + 1) * chans, lanes].astype(F32)
        xs = range(part * WIDE // ROW, (part + 1) * WIDE // ROW)
        keep = jnp.concatenate([row_of(keep_rows, t, x) for x in xs], axis=1)
        jac_val = jnp.concatenate([row_of(jac_rows, t, x) for x in xs], axis=1)
        free = 1.0 - keep
        moved = coupled_val - shift
        scale_cot = free * (cot_val * moved + jac_val)
        values = jnp.concatenate([scale_cot * (1.0 - scale * scale), free * cot_val], axis=0).astype(BF16)
        net[:, p * span + part * WIDE : p * span + (part + 1) * WIDE] = values
        if own:
            growth = jnp.exp(scale)
            sums[0] = sums[0] + values.astype(F32)
            inside = keep * coupled_val + free * moved * jnp.exp(-scale)
            for k, x in enumerate(xs):
                field_in[pl.ds(x * steps + t, chans, stride=rows), :] = inside[:, k * ROW : (k + 1) * ROW]
            gated[:, here] = keep * cot_val + free * cot_val * growth

    convolve(second_w, stack2, acc2, hidden_count, hid, False, finish_net)
    bias2_local = jnp.sum(sums[0], axis=1, keepdims=True)
    for q in range(net_count):
        build_stack(stack3, q * PAD, net[:, q * span : (q + 1) * span], True)

    sums1 = [jnp.zeros((hid, WIDE), F32)]

    def finish_pre(p, part, value):
        h = hidden[:, (p + 2) * span + part * WIDE : (p + 2) * span + (part + 1) * WIDE].astype(F32)
        values = (value * (1.0 - h * h)).astype(BF16)
        sums1[0] = sums1[0] + values.astype(F32)
        base = p * PAD + ROW + part * WIDE
        pre_pad[:, base : base + WIDE] = values
        if part == 0:
            pre_pad[:, p * PAD + (LX + 1) * ROW : (p + 1) * PAD] = values[:, :ROW]
        if part == PARTS - 1:
            pre_pad[:, p * PAD : p * PAD + ROW] = values[:, WIDE - ROW :]
        if p == 0:
            pre_first[:, part * WIDE : (part + 1) * WIDE] = values
        if p == steps - 1:
            pre_last[:, part * WIDE : (part + 1) * WIDE] = values

    convolve(back_w, stack3, acc3, net_count, hid, True, finish_pre)
    bias1_local = jnp.sum(sums1[0], axis=1, keepdims=True)

    def gradient(left, left_row, left_slice, right, right_slice):
        total = None
        for t in range(steps):
            base = (left_slice + t) * PAD
            lhs = jnp.concatenate(
                [left[left_row : left_row + hid, base + (2 - b) * ROW : base + (2 - b) * ROW + span] for b in range(3)],
                axis=0,
            )
            at = (right_slice + t) * PAD + ROW
            term = fast(lhs, right[:, at : at + span], NT)
            total = term if total is None else total + term
        return total

    for a in range(3):
        grad2[a * 3 * hid : (a + 1) * 3 * hid, :] = gradient(stack3, 4 * hid, 1, stack2, 1 + a)
        grad1[a * 3 * hid : (a + 1) * 3 * hid, :] = gradient(pre_pad, 0, 0, stack1, 2 + a)
    tall = 9 * hid
    half = tall // 2
    packed[:tall, :] = grad2[:, :ROW].astype(BF16)
    packed[tall : 2 * tall, :] = grad2[:, ROW : 2 * ROW].astype(BF16)
    packed[2 * tall : 3 * tall, :] = grad1[:, :ROW].astype(BF16)
    packed[3 * tall : 3 * tall + half, :] = jnp.concatenate(
        [
            grad2[:half, 2 * ROW :],
            grad1[:half, ROW:],
            grad2[half:, 2 * ROW :],
            grad1[half:, ROW:],
            jnp.zeros((half, ROW - 2 * hid - 2 * chans), F32),
        ],
        axis=1,
    ).astype(BF16)
    jac_total = jnp.sum(jnp.sum(jac_own, axis=0, keepdims=True), axis=1, keepdims=True)
    small = jnp.concatenate(
        [
            mix_local[...],
            bias1_local[:chans],
            bias1_local[chans:],
            bias2_local[:chans],
            bias2_local[chans:],
            jnp.broadcast_to(jac_total, (chans, 1)),
            jnp.zeros((chans, ROW - chans - 5), F32),
        ],
        axis=1,
    )
    packed[3 * tall + half :, :] = two_part(small).astype(BF16)


def two_part(values):
    high = values.astype(BF16).astype(F32)
    return high + pltpu.roll(values - high, ROW // 2, 1)


def sum_kernel(flag, parts, total):
    value = parts[0].astype(F32)
    for k in range(1, parts.shape[0]):
        value = value + parts[k].astype(F32)
    total[...] = value.astype(BF16)
    last = parts.shape[1] - 16
    tail = value[last:]
    lane = lax.broadcasted_iota(jnp.int32, tail.shape, 1)
    joined = jnp.where(lane < ROW // 2, tail + pltpu.roll(tail, ROW // 2, 1), 0.0)
    total[last:, :] = jnp.where(flag[0] == 1, two_part(joined), tail).astype(BF16)


def back_kernel(steps, pre_first, pre_last, from_prev, from_next, first_back, gated, mask, field_cot, stack, acc):
    chans = gated.shape[0]
    span = LX * ROW
    rows = LX * steps
    keep = mask[...].astype(F32)
    for q, ref in enumerate((from_prev, pre_first, pre_last, from_next)):
        build_stack(stack, q * PAD, ref[...], True)

    def finish(p, part, value):
        here = slice(p * span + part * WIDE, p * span + (part + 1) * WIDE)
        base = gated[:, here]
        for k in range(WIDE // ROW):
            row = (part * WIDE // ROW + k) * steps + p
            lanes = slice(k * ROW, (k + 1) * ROW)
            field_cot[pl.ds(row, chans, stride=rows), :] = base[:, lanes] + keep[row : row + 1] * value[:, lanes]

    convolve(first_back[...], stack, acc, 4, chans, True, finish)


def unpack_kernel(norm, full, perm, lower, upper, logs_row,
                  grad_kern1, grad_bias1, grad_kern2, grad_bias2, grad_lower, grad_upper, grad_logs):
    hid, chans = grad_kern1.shape[1:]
    tall = 9 * hid
    half = tall // 2
    for group in range(9):
        for part in range(hid // 16):
            at = group * hid + part * 16
            one = full[at : at + 16, :].astype(F32) * norm
            two = full[tall + at : tall + at + 16, :].astype(F32) * norm
            three = full[2 * tall + at : 2 * tall + at + 16, :].astype(F32) * norm
            late = at >= half
            spot = 3 * tall + (at - half if late else at)
            four = full[spot : spot + 16, :].astype(F32) * norm
            shift = hid + chans if late else 0
            outs = slice(part * 16, part * 16 + 16)
            for ce in range(9):
                tap = group * 9 + ce
                if ce < 8:
                    source = (one, two)[ce // 4]
                    lane = ce % 4 * hid
                    grad_kern2[tap, outs, :] = source[:, lane : lane + hid]
                    grad_kern1[tap, outs, :] = three[:, ce * chans : (ce + 1) * chans]
                else:
                    grad_kern2[tap, outs, :] = four[:, shift : shift + hid]
                    grad_kern1[tap, outs, :] = four[:, shift + hid : shift + hid + chans]
    tail = full[3 * tall + half :, :].astype(F32)
    small = (tail + pltpu.roll(tail, ROW // 2, 1)) * norm
    perm_t, eye, strict_low, strict_up = mix_parts(perm[...], lower[...], upper[...])
    diag = jnp.exp(logs_row[...])
    mix_grad = exact(perm_t, small[:, :chans], NN)
    lower_full = exact(mix_grad, strict_up + eye * diag, NT)
    low_t = exact(eye, strict_low + eye, NT)
    upper_full = exact(low_t, mix_grad, NN)
    row = lax.broadcasted_iota(jnp.int32, (chans, chans), 0)
    col = lax.broadcasted_iota(jnp.int32, (chans, chans), 1)
    grad_lower[...] = jnp.where(row > col, lower_full, 0.0)
    grad_upper[...] = jnp.where(row < col, upper_full, 0.0)

    def across(column):
        return jnp.sum(eye * column, axis=0, keepdims=True)

    jac_total = small[:1, chans + 4 : chans + 5]
    grad_logs[...] = jnp.sum(eye * upper_full, axis=0, keepdims=True) * diag + jac_total
    bias = [across(small[:, chans + k : chans + k + 1]) for k in range(4)]
    grad_bias1[:, :chans] = bias[0]
    grad_bias1[:, chans:] = bias[1]
    grad_bias2[:, :chans] = bias[2]
    grad_bias2[:, chans:] = bias[3]


def ring(amount):
    count = lax.axis_size("ta")
    return [(i, (i + amount) % count) for i in range(count)]


def flat(field, steps):
    chans = field.shape[0]
    return field.reshape(chans, steps, LX, ROW).transpose(0, 2, 1, 3).reshape(chans * LX * steps, ROW)


def body(out_field, out_cot, jac_cot, mask, perm, lower_param, upper_param, log_scale, kern1, bias1, kern2, bias2):
    chans, steps, site_count = out_field.shape
    hid = bias1.shape[0]
    assert steps == 2 and site_count == LX * ROW and hid == 2 * chans == 32
    count = lax.axis_size("ta")
    span = LX * ROW
    perm_row = perm[None]
    logs_row = log_scale[None]
    logs_col = log_scale[:, None]
    jac_rows = flat(jac_cot[None], steps)
    mask_rows = flat(mask[None], steps)
    own = shape((chans, steps * span))
    pack_shape = shape(((steps + 1) * chans, span + ROW), BF16)
    edge_shape = shape((chans, span), BF16)
    coupled, cot, pack_up, pack_down, edge_last, edge_first, mix_local = vmem_call(
        functools.partial(mix_kernel, steps),
        (own, own, pack_shape, pack_shape, edge_shape, edge_shape, shape((chans, chans))),
        (perm_row, lower_param, upper_param, logs_row, logs_col, flat(out_field, steps), flat(out_cot, steps), jac_rows, mask_rows),
        10**7,
    )
    from_prev = lax.ppermute(pack_up, "ta", ring(1))
    from_next = lax.ppermute(pack_down, "ta", ring(-1))
    from_prev2 = lax.ppermute(edge_last, "ta", ring(2))
    from_next2 = lax.ppermute(edge_first, "ta", ring(-2))
    first, second, first_back, second_back = vmem_call(
        weight_kernel,
        (
            shape((3 * hid, 27 * chans), BF16),
            shape((3 * hid, 27 * hid), BF16),
            shape((3 * chans, 27 * hid), BF16),
            shape((3 * hid, 27 * hid), BF16),
        ),
        (kern1, kern2),
        10**8,
    )
    hidden_count = 3 * steps
    field_in, gated, pre_first, pre_last, packed = vmem_call(
        functools.partial(main_kernel, steps),
        (
            shape((chans * LX * steps, ROW)),
            own,
            shape((hid, span), BF16),
            shape((hid, span), BF16),
            shape((1024, ROW), BF16),
        ),
        (coupled, cot, jac_rows, mask_rows, from_prev, from_next, from_prev2, from_next2,
         first, second, second_back, bias1[:, None], bias2[:, None], mix_local),
        3 * 10**9,
        scratch=[
            pltpu.VMEM((9 * chans, (hidden_count + 2) * PAD), BF16),
            pltpu.VMEM((9 * hid, hidden_count * PAD), BF16),
            pltpu.VMEM((9 * hid, (hidden_count - 2) * PAD), BF16),
            pltpu.VMEM((hid, steps * PAD), BF16),
            pltpu.VMEM((hid, hidden_count * span), BF16),
            pltpu.VMEM((hid, (hidden_count - 2) * span), BF16),
            pltpu.VMEM((hid, hidden_count * span), F32),
            pltpu.VMEM((hid, (hidden_count - 2) * span), F32),
            pltpu.VMEM((hid, steps * span), F32),
            pltpu.VMEM((9 * hid, 9 * chans), F32),
            pltpu.VMEM((9 * hid, 9 * hid), F32),
        ],
    )
    pre_prev = lax.ppermute(pre_last, "ta", ring(1))
    pre_next = lax.ppermute(pre_first, "ta", ring(-1))
    scattered = lax.all_to_all(packed.reshape(count, 1024 // count, ROW), "ta", 0, 0, tiled=True)
    flag = (lax.axis_index("ta") == count - 1).astype(jnp.int32).reshape(1)
    total = pl.pallas_call(
        sum_kernel,
        out_shape=shape((1024 // count, ROW), BF16),
        in_specs=[pl.BlockSpec(memory_space=pltpu.SMEM), pl.BlockSpec(memory_space=pltpu.VMEM)],
        out_specs=pl.BlockSpec(memory_space=pltpu.VMEM),
    )(flag, scattered)
    full = lax.all_to_all(jnp.broadcast_to(total[None], scattered.shape), "ta", 0, 0, tiled=True).reshape(1024, ROW)
    field_cot = vmem_call(
        functools.partial(back_kernel, steps),
        shape((chans * LX * steps, ROW)),
        (pre_first, pre_last, pre_prev, pre_next, first_back, gated, mask_rows),
        4 * 10**8,
        scratch=[pltpu.VMEM((9 * hid, (steps + 2) * PAD), BF16), pltpu.VMEM((chans, steps * span), F32)],
    )
    norm = 1.0 / math.sqrt(steps * site_count * count)
    grads = vmem_call(
        functools.partial(unpack_kernel, norm),
        (
            shape(kern1.shape), shape((1, hid)), shape(kern2.shape), shape((1, hid)),
            shape((chans, chans)), shape((chans, chans)), shape((1, chans)),
        ),
        (full, perm_row, lower_param, upper_param, logs_row),
        10**6,
    )

    def unflat(rows):
        return rows.reshape(chans, LX, steps, ROW).transpose(0, 2, 1, 3).reshape(chans, steps, site_count)

    grad_kern1, grad_bias1, grad_kern2, grad_bias2, grad_lower, grad_upper, grad_logs = grads
    return (
        unflat(field_in), unflat(field_cot), grad_kern1, grad_bias1[0], grad_kern2, grad_bias2[0],
        grad_lower, grad_upper, grad_logs[0],
    )


def solution(mesh):
    split = ("groups", "ta")
    in_specs = (P(None, split, None), P(None, split, None), P(split, None), P(split, None)) + (P(),) * 8
    out_specs = (
        P(None, split, None),
        P(None, split, None),
        P("groups", None, None),
        P("groups"),
        P("groups", None, None),
        P("groups"),
        P("groups", None),
        P("groups", None),
        P("groups"),
    )
    return jax.shard_map(body, mesh=mesh, in_specs=in_specs, out_specs=out_specs, check_vma=False)
```

```python
import functools
import math

import jax
import jax.numpy as jnp
from jax import lax
from jax.experimental import pallas as pl
from jax.experimental.pallas import tpu as pltpu
from jax.sharding import PartitionSpec as P


LX = 8
LY = 8
LZ = 16
ROW = LY * LZ
PAD = (LX + 2) * ROW

HIGH = lax.Precision.HIGHEST
F32 = jnp.float32
BF16 = jnp.bfloat16


NN = (((1,), (0,)), ((), ()))
NT = (((1,), (1,)), ((), ()))


def exact(a, b, dims):
    return lax.dot_general(a, b, dims, precision=HIGH, preferred_element_type=F32)


def fast(a, b, dims):
    return lax.dot_general(a, b, dims, preferred_element_type=F32)


def vmem_call(kernel, out_shape, args, flops, scratch=(), scalar=None):
    spec = pl.BlockSpec(memory_space=pltpu.VMEM)
    first = [] if scalar is None else [scalar]
    moved = sum(a.size * a.dtype.itemsize for a in args)
    return pl.pallas_call(
        kernel,
        out_shape=out_shape,
        in_specs=[pl.BlockSpec(memory_space=pltpu.SMEM)] * len(first) + [spec] * len(args),
        out_specs=jax.tree.map(lambda _: spec, out_shape),
        scratch_shapes=list(scratch),
        compiler_params=pltpu.CompilerParams(vmem_limit_bytes=40 << 20),
        cost_estimate=pl.CostEstimate(flops=flops, bytes_accessed=moved, transcendentals=0),
    )(*first, *args)


def shape(dims, dtype=F32):
    return jax.ShapeDtypeStruct(dims, dtype)


def mix_parts(perm, lower, upper):
    count = lower.shape[0]
    row = lax.broadcasted_iota(jnp.int32, (count, count), 0)
    col = lax.broadcasted_iota(jnp.int32, (count, count), 1)
    perm_t = (row == perm).astype(F32)
    eye = (row == col).astype(F32)
    strict_low = jnp.where(row > col, lower, 0.0)
    strict_up = jnp.where(row < col, upper, 0.0)
    return perm_t, eye, strict_low, strict_up


def mix_kernel(steps, *refs):
    count = 12
    sources, (coupled, cot, pack_up, pack_down, edge_last, edge_first, mix_local, aux, columns, kern1, kern2) = (
        refs[:count], refs[count : 2 * count - 1]
    )
    (perm, lower, upper, logs_row, bias1, bias2, out_field, out_cot, jac, mask), sems = refs[2 * count - 1 : -1], refs[-1]
    targets = (perm, lower, upper, logs_row, bias1, bias2, jac, mask, out_cot, out_field)
    sources = sources[:6] + (sources[8], sources[9], sources[7], sources[6]) + sources[10:]
    copies = [
        pltpu.make_async_copy(source, target, sems.at[k])
        for k, (source, target) in enumerate(zip(sources, targets + (kern1, kern2)))
    ]
    for copy in copies:
        copy.start()
    for copy in copies[:4]:
        copy.wait()
    chans = lower.shape[0]
    perm_t, eye, strict_low, strict_up = mix_parts(perm[...], lower[...], upper[...])
    logs_col = jnp.sum(eye * logs_row[...], axis=1, keepdims=True)
    inv_diag = 1.0 / jnp.exp(logs_col)
    solve = perm_t
    for j in range(chans - 1):
        solve = solve - strict_low[:, j : j + 1] * solve[j : j + 1, :]
    solve = solve * inv_diag
    scaled = strict_up * inv_diag
    for j in range(chans - 1, 0, -1):
        solve = solve - scaled[:, j : j + 1] * solve[j : j + 1, :]
    upper_tri = strict_up + eye * jnp.exp(logs_row[...])
    low_up = exact(strict_low + eye, upper_tri, NN)
    low_up_t = exact(eye, low_up, NT)
    perm_mat_t = exact(low_up_t, perm_t, NN)

    def gather(ref):
        return jnp.concatenate(
            [
                ref[pl.ds(x * steps + t, chans, stride=LX * steps), :]
                for t in range(steps)
                for x in range(LX)
            ],
            axis=1,
        )

    for copy in copies[4:10]:
        copy.wait()
    cot_in = gather(out_cot)
    coupled_val = exact(solve, gather(out_field), NN)
    cot_val = exact(perm_mat_t, cot_in, NN)
    coupled[...] = coupled_val
    cot[...] = cot_val
    mix_local[...] = exact(cot_in, coupled_val, NT)
    keep = mask[...].astype(F32)
    span = LX * ROW
    for t in range(steps):
        block = coupled_val[:, t * span : (t + 1) * span].astype(BF16)
        pack_up[t * chans : (t + 1) * chans, :span] = block
        pack_down[t * chans : (t + 1) * chans, :span] = block
    top = steps * chans
    pack_up[top : top + chans, :span] = cot_val[:, (steps - 1) * span :].astype(BF16)
    pack_down[top : top + chans, :span] = cot_val[:, :span].astype(BF16)
    jac_val = jac[...]
    aux[: LX * steps, :] = keep
    aux[LX * steps :, :] = jac_val
    jac_hi = jac_val.astype(BF16)
    jac_lo = (jac_val - jac_hi.astype(F32)).astype(BF16)
    rows = LX * steps
    for pack in (pack_up, pack_down):
        pack[:rows, span:] = jac_hi
        pack[rows : 2 * rows, span:] = jac_lo
        pack[2 * rows : 3 * rows, span:] = keep.astype(BF16)
    for t, edge in ((steps - 1, edge_last), (0, edge_first)):
        for x in range(LX):
            at = t * span + x * ROW
            row = x * steps + t
            edge[:, x * ROW : (x + 1) * ROW] = (keep[row : row + 1] * coupled_val[:, at : at + ROW]).astype(BF16)
    columns[...] = jnp.concatenate([column_of(bias1[...]), column_of(bias2[...])], axis=1)
    for copy in copies[10:]:
        copy.wait()


def column_of(row):
    size = row.shape[1]
    eye = lax.broadcasted_iota(jnp.int32, (size, size), 0) == lax.broadcasted_iota(jnp.int32, (size, size), 1)
    return jnp.sum(jnp.where(eye, row, 0.0), axis=1, keepdims=True)


def identity(size):
    row = lax.broadcasted_iota(jnp.int32, (size, size), 0)
    col = lax.broadcasted_iota(jnp.int32, (size, size), 1)
    return (row == col).astype(BF16)


def weight_kernel(kern1, kern2, first, second, first_back, second_back, plain1, plain2):
    for kern, plain, forward, backward in (
        (kern1, plain1, first, first_back),
        (kern2, plain2, second, second_back),
    ):
        count = kern.shape[1]
        i = plain.shape[1]
        o = kern.shape[0] // i
        across = fast(identity(count), kern[...], NT)
        for k in range(o):
            plain[pl.ds(k, count, stride=o), :] = across[:, k * i : (k + 1) * i]
        for a in range(3):
            for j in range(27):
                tap = a * 27 + j
                forward[a * o : (a + 1) * o, j * i : (j + 1) * i] = plain[tap * o : (tap + 1) * o, :].astype(BF16)
            block = plain[a * 27 * o : (a + 1) * 27 * o, :].astype(BF16)
            backward[a * i : (a + 1) * i, :] = fast(identity(i), block, NT).astype(BF16)


def build_stack(stack, base, values, flip):
    chans = values.shape[0]
    tall = jnp.concatenate([values[:, x * ROW : (x + 1) * ROW] for x in range(LX)], axis=0)
    z = lax.broadcasted_iota(jnp.int32, tall.shape, 1) % LZ
    before = jnp.where(z == 0, pltpu.roll(tall, ROW - (LZ - 1), 1), pltpu.roll(tall, 1, 1))
    after = jnp.where(z == LZ - 1, pltpu.roll(tall, LZ - 1, 1), pltpu.roll(tall, ROW - 1, 1))
    for e, along_z in enumerate((before, tall, after)):
        for c, amount in enumerate((LZ, 0, ROW - LZ)):
            moved = pltpu.roll(along_z, amount, 1) if amount else along_z
            at = c * 3 + e
            at = (8 - at if flip else at) * chans
            for x in range(LX):
                block = moved[x * chans : (x + 1) * chans]
                spots = [x + 1] + ([LX + 1] if x == 0 else []) + ([0] if x == LX - 1 else [])
                for spot in spots:
                    stack[at : at + chans, base + spot * ROW : base + (spot + 1) * ROW] = block


WIDE = 256
PARTS = LX * ROW // WIDE
EARLY = 5


def taps(weights, stack, base, part, flip):
    order = (2, 1, 0) if flip else (0, 1, 2)
    start = base + part * WIDE
    block = jnp.concatenate([stack[:, start + b * ROW : start + b * ROW + WIDE] for b in order], axis=0)
    return fast(weights, block, NN)


def convolve(weights, stack, acc, count, outs, flip, finish):
    span = LX * ROW
    for q in range(count):
        for part in range(PARTS):
            all_taps = taps(weights, stack, q * PAD, part, flip)
            groups = [all_taps[a * outs : (a + 1) * outs] for a in range(3)]
            if flip:
                groups = groups[::-1]
            for a, group in enumerate(groups):
                p = q - a
                if 0 <= p <= count - 3:
                    where = slice(p * span + part * WIDE, p * span + (part + 1) * WIDE)
                    if a == 0:
                        acc[:, where] = group
                    elif a == 1:
                        acc[:, where] = acc[:, where] + group
                    else:
                        finish(p, part, acc[:, where] + group)


def main_kernel(steps, core, coupled, cot, aux, columns, from_prev, from_next, from_prev2, from_next2,
                first, second, second_back, mix_local,
                field_in, gated, pre_first, pre_last, mine, other,
                stack1, stack2, stack3, pre_pad, hidden, net, acc1, acc2, acc3, grad1, grad2):
    chans = coupled.shape[0]
    hid = columns.shape[0]
    span = LX * ROW
    rows = LX * steps
    keep_own = aux[:rows, :]
    jac_own = aux[rows:, :]
    sides = {}
    for name, pack in (("prev", from_prev), ("next", from_next)):
        keep = pack[2 * rows : 3 * rows, span:].astype(F32)
        jac_side = pack[:rows, span:].astype(F32) + pack[rows : 2 * rows, span:].astype(F32)
        sides[name] = (pack, keep, jac_side)

    def row_of(block, t, x):
        return block[x * steps + t : x * steps + t + 1]

    def masked(values, keep, t):
        return jnp.concatenate(
            [(row_of(keep, t, x) * values[:, x * ROW : (x + 1) * ROW]).astype(BF16) for x in range(LX)], axis=1
        )

    first_w = first[...]
    second_w = second[...]
    back_w = second_back[...]
    slices = [from_prev2[...]]
    for t in range(steps):
        slices.append(masked(from_prev[t * chans : (t + 1) * chans, :span].astype(F32), sides["prev"][1], t))
    for t in range(steps):
        slices.append(masked(coupled[:, t * span : (t + 1) * span], keep_own, t))
    for t in range(steps):
        slices.append(masked(from_next[t * chans : (t + 1) * chans, :span].astype(F32), sides["next"][1], t))
    slices.append(from_next2[...])
    for q, values in enumerate(slices):
        build_stack(stack1, q * PAD, values, False)

    offset1 = columns[:, :1]

    def finish_hidden(p, part, value):
        hidden[:, p * span + part * WIDE : p * span + (part + 1) * WIDE] = jnp.tanh(value + offset1).astype(BF16)

    convolve(first_w, stack1, acc1, len(slices), hid, False, finish_hidden)
    hidden_count = len(slices) - 2
    for q in range(hidden_count):
        build_stack(stack2, q * PAD, hidden[:, q * span : (q + 1) * span], False)

    offset2 = columns[:, 1:2]
    net_count = hidden_count - 2
    sums = [jnp.zeros((2 * chans, WIDE), F32)]

    def finish_net(p, part, value):
        value = value + offset2
        scale = jnp.tanh(value[:chans])
        shift = value[chans:]
        lanes = slice(part * WIDE, (part + 1) * WIDE)
        own = 1 <= p <= steps
        if own:
            t = p - 1
            here = slice(t * span + part * WIDE, t * span + (part + 1) * WIDE)
            coupled_val, cot_val = coupled[:, here], cot[:, here]
            keep_rows, jac_rows = keep_own, jac_own
        else:
            pack, keep_rows, jac_rows = sides["prev" if p == 0 else "next"]
            t = steps - 1 if p == 0 else 0
            coupled_val = pack[t * chans : (t + 1) * chans, lanes].astype(F32)
            cot_val = pack[steps * chans : (steps + 1) * chans, lanes].astype(F32)
        xs = range(part * WIDE // ROW, (part + 1) * WIDE // ROW)
        keep = jnp.concatenate([row_of(keep_rows, t, x) for x in xs], axis=1)
        jac_val = jnp.concatenate([row_of(jac_rows, t, x) for x in xs], axis=1)
        free = 1.0 - keep
        moved = coupled_val - shift
        scale_cot = free * (cot_val * moved + jac_val)
        values = jnp.concatenate([scale_cot * (1.0 - scale * scale), free * cot_val], axis=0).astype(BF16)
        net[:, p * span + part * WIDE : p * span + (part + 1) * WIDE] = values
        if own:
            growth = jnp.exp(scale)
            sums[0] = sums[0] + values.astype(F32)
            inside = keep * coupled_val + free * moved * jnp.exp(-scale)
            for k, x in enumerate(xs):
                field_in[pl.ds(x * steps + t, chans, stride=rows), :] = inside[:, k * ROW : (k + 1) * ROW]
            gated[:, here] = keep * cot_val + free * cot_val * growth

    convolve(second_w, stack2, acc2, hidden_count, hid, False, finish_net)
    bias2_local = jnp.sum(sums[0], axis=1, keepdims=True)
    for q in range(net_count):
        build_stack(stack3, q * PAD, net[:, q * span : (q + 1) * span], True)

    sums1 = [jnp.zeros((hid, WIDE), F32)]

    def finish_pre(p, part, value):
        h = hidden[:, (p + 2) * span + part * WIDE : (p + 2) * span + (part + 1) * WIDE].astype(F32)
        values = (value * (1.0 - h * h)).astype(BF16)
        sums1[0] = sums1[0] + values.astype(F32)
        base = p * PAD + ROW + part * WIDE
        pre_pad[:, base : base + WIDE] = values
        if part == 0:
            pre_pad[:, p * PAD + (LX + 1) * ROW : (p + 1) * PAD] = values[:, :ROW]
        if part == PARTS - 1:
            pre_pad[:, p * PAD : p * PAD + ROW] = values[:, WIDE - ROW :]
        if p == 0:
            pre_first[:, part * WIDE : (part + 1) * WIDE] = values
        if p == steps - 1:
            pre_last[:, part * WIDE : (part + 1) * WIDE] = values

    convolve(back_w, stack3, acc3, net_count, hid, True, finish_pre)
    bias1_local = jnp.sum(sums1[0], axis=1, keepdims=True)

    def gradient(left, left_row, left_slice, right, right_slice):
        total = None
        for t in range(steps):
            base = (left_slice + t) * PAD
            lhs = jnp.concatenate(
                [left[left_row : left_row + hid, base + (2 - b) * ROW : base + (2 - b) * ROW + span] for b in range(3)],
                axis=0,
            )
            at = (right_slice + t) * PAD + ROW
            term = fast(lhs, right[:, at : at + span], NT)
            total = term if total is None else total + term
        return total

    for a in range(3):
        grad2[a * 3 * hid : (a + 1) * 3 * hid, :] = gradient(stack3, 4 * hid, 1, stack2, 1 + a)
        grad1[a * 3 * hid : (a + 1) * 3 * hid, :] = gradient(pre_pad, 0, 0, stack1, 2 + a)
    quarter = hid // 2
    late = EARLY * quarter

    def half_rows(h):
        rows_of = [slice(g * hid + h * quarter, g * hid + (h + 1) * quarter) for g in range(9)]
        rest = jnp.concatenate(
            [jnp.concatenate([grad2[r, 2 * ROW :], grad1[r, ROW:]], axis=1) for r in rows_of], axis=0
        )
        gap = jnp.zeros((2 * late - rest.shape[0], rest.shape[1]), F32)
        rest = jnp.concatenate(
            [rest[:late], jnp.concatenate([rest[late:], gap], axis=0), jnp.zeros((late, ROW - 2 * rest.shape[1]), F32)],
            axis=1,
        )
        blocks = [grad2[r, :ROW] for r in rows_of] + [grad2[r, ROW : 2 * ROW] for r in rows_of]
        return jnp.concatenate(blocks + [grad1[r, :ROW] for r in rows_of] + [rest], axis=0)

    low, high = half_rows(0), half_rows(1)
    upper_core = core[0] == 1
    size = low.shape[0]
    mine[:size, :] = jnp.where(upper_core, high, low).astype(BF16)
    other[:size, :] = jnp.where(upper_core, low, high).astype(BF16)
    jac_total = jnp.sum(jnp.sum(jac_own, axis=0, keepdims=True), axis=1, keepdims=True)
    small = jnp.concatenate(
        [
            mix_local[...],
            bias1_local[:chans],
            bias1_local[chans:],
            bias2_local[:chans],
            bias2_local[chans:],
            jnp.broadcast_to(jac_total, (chans, 1)),
            jnp.zeros((chans, ROW - chans - 5), F32),
        ],
        axis=1,
    )
    small = two_part(small).astype(BF16)
    mine[size:, :] = small
    other[size:, :] = small


def two_part(values):
    high = values.astype(BF16).astype(F32)
    return high + pltpu.roll(values - high, ROW // 2, 1)


def join_parts(tail):
    lane = lax.broadcasted_iota(jnp.int32, tail.shape, 1)
    return jnp.where(lane < ROW // 2, tail + pltpu.roll(tail, ROW // 2, 1), 0.0)


def sum_kernel(left, right, total):
    value = left[...].astype(F32) + right[...].astype(F32)
    last = value.shape[0] - 16
    total[:last, :] = value[:last].astype(BF16)
    total[last:, :] = two_part(join_parts(value[last:])).astype(BF16)


def back_kernel(steps, pre_first, pre_last, from_prev, from_next, first_back, gated, aux, field_cot, stack, acc):
    chans = gated.shape[0]
    span = LX * ROW
    rows = LX * steps
    keep = aux[:rows, :]
    for q, ref in enumerate((from_prev, pre_first, pre_last, from_next)):
        build_stack(stack, q * PAD, ref[...], True)

    def finish(p, part, value):
        here = slice(p * span + part * WIDE, p * span + (part + 1) * WIDE)
        base = gated[:, here]
        for k in range(WIDE // ROW):
            row = (part * WIDE // ROW + k) * steps + p
            lanes = slice(k * ROW, (k + 1) * ROW)
            field_cot[pl.ds(row, chans, stride=rows), :] = base[:, lanes] + keep[row : row + 1] * value[:, lanes]

    convolve(first_back[...], stack, acc, 4, chans, True, finish)


def unpack(norm, source, plain1, plain2, wide, outs):
    chans, hid = plain1.shape[1], plain2.shape[1]
    size = plain1.shape[0] // 81
    tall = 9 * size
    for group in range(9):
        at = group * size
        one, two, three = (source[k * tall + at : k * tall + at + size, :].astype(F32) for k in range(3))
        late = group >= EARLY
        spot = 3 * tall + at - (EARLY * size if late else 0)
        four = source[spot : spot + size, :].astype(F32)
        shift = hid + chans if late else 0
        for ce in range(9):
            where = (group * 9 + ce) * size
            rows = slice(where, where + size)
            if ce < 8:
                lane = ce % 4 * hid
                plain2[rows, :] = (one, two)[ce // 4][:, lane : lane + hid]
                plain1[rows, :] = three[:, ce * chans : (ce + 1) * chans]
            else:
                plain2[rows, :] = four[:, shift : shift + hid]
                plain1[rows, :] = four[:, shift + hid : shift + hid + chans]
    for plain, (out, base) in zip((plain1, plain2), outs):
        per = ROW // plain.shape[1]
        for group in range(size // per):
            pieces = [plain[pl.ds(group * per + k, 81, stride=size), :] for k in range(per)]
            wide[:81, :] = jnp.concatenate(pieces, axis=1) * norm
            out[pl.ds(base + group * ROW, ROW), :] = wide[...].T[:, :81]


def own_kernel(norm, source, perm, lower, upper, logs_row,
               grad_kern1, grad_bias1, grad_kern2, grad_bias2, grad_lower, grad_upper, grad_logs,
               plain1, plain2, wide):
    chans = plain1.shape[1]
    unpack(norm, source, plain1, plain2, wide, ((grad_kern1, 0), (grad_kern2, 0)))
    small = join_parts(source[source.shape[0] - 16 :, :].astype(F32)) * norm
    perm_t, eye, strict_low, strict_up = mix_parts(perm[...], lower[...], upper[...])
    diag = jnp.exp(logs_row[...])
    mix_grad = exact(perm_t, small[:, :chans], NN)
    lower_full = exact(mix_grad, strict_up + eye * diag, NT)
    low_t = exact(eye, strict_low + eye, NT)
    upper_full = exact(low_t, mix_grad, NN)
    row = lax.broadcasted_iota(jnp.int32, (chans, chans), 0)
    col = lax.broadcasted_iota(jnp.int32, (chans, chans), 1)
    grad_lower[...] = jnp.where(row > col, lower_full, 0.0)
    grad_upper[...] = jnp.where(row < col, upper_full, 0.0)

    def across(column):
        return jnp.sum(eye * column, axis=0, keepdims=True)

    jac_total = small[:1, chans + 4 : chans + 5]
    grad_logs[...] = jnp.sum(eye * upper_full, axis=0, keepdims=True) * diag + jac_total
    bias = [across(small[:, chans + k : chans + k + 1]) for k in range(4)]
    grad_bias1[:, :chans] = bias[0]
    grad_bias1[:, chans:] = bias[1]
    grad_bias2[:, :chans] = bias[2]
    grad_bias2[:, chans:] = bias[3]


def other_kernel(norm, core, source, own1, own2, grad_kern1, grad_kern2, plain1, plain2, wide):
    outs = []
    for own, out in ((own1, grad_kern1), (own2, grad_kern2)):
        size = own.shape[0]
        out[pl.ds(pl.multiple_of(core[0] * size, ROW), size), :] = own[...]
        outs.append((out, pl.multiple_of((1 - core[0]) * size, ROW)))
    unpack(norm, source, plain1, plain2, wide, outs)


def ring(amount):
    count = lax.axis_size("ta")
    return [(i, (i + amount) % count) for i in range(count)]


def flat(field, steps):
    chans = field.shape[0]
    return field.reshape(chans, steps, LX, ROW).transpose(0, 2, 1, 3).reshape(chans * LX * steps, ROW)


def body(out_field, out_cot, jac_cot, mask, perm, lower_param, upper_param, log_scale, kern1, bias1, kern2, bias2):
    chans, steps, site_count = out_field.shape
    hid = bias1.shape[0]
    assert steps == 2 and site_count == LX * ROW and hid == 2 * chans == 32
    count = lax.axis_size("ta")
    span = LX * ROW
    perm_row = perm[None]
    logs_row = log_scale[None]
    own = shape((chans, steps * span))
    pack_shape = shape(((steps + 1) * chans, span + ROW), BF16)
    edge_shape = shape((chans, span), BF16)
    kern1_rows = kern1.transpose(1, 2, 0).reshape(hid * chans, kern1.shape[0])
    kern2_rows = kern2.transpose(1, 2, 0).reshape(hid * hid, kern2.shape[0])
    inputs = (
        perm_row, lower_param, upper_param, logs_row, bias1[None], bias2[None],
        flat(out_field, steps), flat(out_cot, steps), flat(jac_cot[None], steps), flat(mask[None], steps),
        kern1_rows, kern2_rows,
    )
    outputs = (
        own, own, pack_shape, pack_shape, edge_shape, edge_shape, shape((chans, chans)),
        shape((2 * LX * steps, ROW)), shape((hid, 2)), shape(kern1_rows.shape, BF16), shape(kern2_rows.shape, BF16),
    )
    coupled, cot, pack_up, pack_down, edge_last, edge_first, mix_local, aux, columns, kern1_near, kern2_near = pl.pallas_call(
        functools.partial(mix_kernel, steps),
        out_shape=outputs,
        in_specs=[pl.BlockSpec(memory_space=pltpu.HBM)] * len(inputs),
        out_specs=tuple(pl.BlockSpec(memory_space=pltpu.VMEM) for _ in outputs),
        scratch_shapes=[pltpu.VMEM(a.shape, a.dtype) for a in inputs[:10]] + [pltpu.SemaphoreType.DMA((len(inputs),))],
        compiler_params=pltpu.CompilerParams(vmem_limit_bytes=40 << 20),
        cost_estimate=pl.CostEstimate(flops=10**7, bytes_accessed=10**6, transcendentals=0),
    )(*[pltpu.with_memory_space_constraint(a, pltpu.HBM) for a in inputs])
    from_prev = lax.ppermute(pack_up, "ta", ring(1))
    from_prev2 = lax.ppermute(edge_last, "ta", ring(2))
    from_next = lax.ppermute(pack_down, "ta", ring(-1))
    from_next2 = lax.ppermute(edge_first, "ta", ring(-2))
    first, second, first_back, second_back = vmem_call(
        weight_kernel,
        (
            shape((3 * hid, 27 * chans), BF16),
            shape((3 * hid, 27 * hid), BF16),
            shape((3 * chans, 27 * hid), BF16),
            shape((3 * hid, 27 * hid), BF16),
        ),
        (kern1_near, kern2_near),
        10**8,
        scratch=[pltpu.VMEM((81 * hid, chans), F32), pltpu.VMEM((81 * hid, hid), F32)],
    )
    hidden_count = 3 * steps
    core = (lax.axis_index("ta") % 2).astype(jnp.int32).reshape(1)
    half_size = (3 * 9 + EARLY) * (hid // 2) + 16
    half_shape = shape((half_size, ROW), BF16)
    field_in, gated, pre_first, pre_last, mine, other = vmem_call(
        functools.partial(main_kernel, steps),
        (
            shape((chans * LX * steps, ROW)),
            own,
            shape((hid, span), BF16),
            shape((hid, span), BF16),
            half_shape,
            half_shape,
        ),
        (coupled, cot, aux, columns, from_prev, from_next, from_prev2, from_next2,
         first, second, second_back, mix_local),
        3 * 10**9,
        scratch=[
            pltpu.VMEM((9 * chans, (hidden_count + 2) * PAD), BF16),
            pltpu.VMEM((9 * hid, hidden_count * PAD), BF16),
            pltpu.VMEM((9 * hid, (hidden_count - 2) * PAD), BF16),
            pltpu.VMEM((hid, steps * PAD), BF16),
            pltpu.VMEM((hid, hidden_count * span), BF16),
            pltpu.VMEM((hid, (hidden_count - 2) * span), BF16),
            pltpu.VMEM((hid, hidden_count * span), F32),
            pltpu.VMEM((hid, (hidden_count - 2) * span), F32),
            pltpu.VMEM((hid, steps * span), F32),
            pltpu.VMEM((9 * hid, 9 * chans), F32),
            pltpu.VMEM((9 * hid, 9 * hid), F32),
        ],
        scalar=core,
    )

    def swap(values, bit):
        return lax.ppermute(values, "ta", [(i, i ^ bit) for i in range(count)])

    def add(left, right):
        return vmem_call(sum_kernel, half_shape, (left, right), 10**5)

    total = add(mine, swap(other, 1))
    bit = 2
    while bit < count:
        total = add(total, swap(total, bit))
        bit = 2 * bit
    rest = swap(total, 1)
    pre_prev = lax.ppermute(pre_last, "ta", ring(1))
    pre_next = lax.ppermute(pre_first, "ta", ring(-1))
    field_cot = vmem_call(
        functools.partial(back_kernel, steps),
        shape((chans * LX * steps, ROW)),
        (pre_first, pre_last, pre_prev, pre_next, first_back, gated, aux),
        4 * 10**8,
        scratch=[pltpu.VMEM((9 * hid, (steps + 2) * PAD), BF16), pltpu.VMEM((chans, steps * span), F32)],
    )
    norm = 1.0 / math.sqrt(steps * site_count * count)
    scratch = [
        pltpu.VMEM((81 * hid // 2, chans), F32),
        pltpu.VMEM((81 * hid // 2, hid), F32),
        pltpu.VMEM((ROW, ROW), F32),
    ]
    own1, grad_bias1, own2, grad_bias2, grad_lower, grad_upper, grad_logs = vmem_call(
        functools.partial(own_kernel, norm),
        (
            shape((hid * chans // 2, 81)), shape((1, hid)), shape((hid * hid // 2, 81)), shape((1, hid)),
            shape((chans, chans)), shape((chans, chans)), shape((1, chans)),
        ),
        (total, perm_row, lower_param, upper_param, logs_row),
        10**6,
        scratch=scratch,
    )
    grad_kern1, grad_kern2 = vmem_call(
        functools.partial(other_kernel, norm),
        (shape(kern1_rows.shape), shape(kern2_rows.shape)),
        (rest, own1, own2),
        10**6,
        scratch=scratch,
        scalar=core,
    )

    def unflat(rows):
        return rows.reshape(chans, LX, steps, ROW).transpose(0, 2, 1, 3).reshape(chans, steps, site_count)

    return (
        unflat(field_in), unflat(field_cot),
        grad_kern1.reshape(hid, chans, -1).transpose(2, 0, 1), grad_bias1[0],
        grad_kern2.reshape(hid, hid, -1).transpose(2, 0, 1), grad_bias2[0],
        grad_lower, grad_upper, grad_logs[0],
    )


def solution(mesh):
    split = ("groups", "ta")
    in_specs = (P(None, split, None), P(None, split, None), P(split, None), P(split, None)) + (P(),) * 8
    out_specs = (
        P(None, split, None),
        P(None, split, None),
        P("groups", None, None),
        P("groups"),
        P("groups", None, None),
        P("groups"),
        P("groups", None),
        P("groups", None),
        P("groups"),
    )

    return jax.shard_map(body, mesh=mesh, in_specs=in_specs, out_specs=out_specs, check_vma=False)
```
